32 devices in a mesh: grp: 2 (over y), wide: 8 (over z, x), tm: 2 (over core).
Axes of the slice: x: 2, y: 2, z: 4, core: 2. Of those that a mesh axis runs over, the one named last changes fastest.
Arguments:
- voltages: bfloat16 [2048, 65536], P('wide', ('grp', 'tm')), parts along dimension 1, may hold values from -6 to 6
- channels: int32 [16], replicated, may hold values from 0 to 1023, as said below
- tile_pairs: int32 [128, 2], replicated, may hold values from 0 to 31, as said below
Outputs:
- visibility: bfloat16 [32, 128, 64, 128], P(('grp', 'wide', 'tm')), parts along dimension 0
The draws below stay inside these ranges and needn't reach their ends.
There are 2 independent parts, one for each index of `grp`. The reference program is written for one: setup_inputs(seed, part) draws one part's arguments, and reference() takes and returns one part's arrays. A program takes and returns all parts, laid end to end along the dimension named above; an argument that names none is the same for every part. Nothing has to cross between parts.
Inputs may be any that keep to these rules, and one draw needn't show every extreme that they name: `channels`: 16 different channel numbers in no fixed order; 0 and 1023 are always among them. `tile_pairs`: 128 different ordered tile pairs; (0, 0) and (31, 31) are always among them.
All inputs are finite; a program needn't handle non-finite values.
Results may differ from the reference program's by a relative error of at most 0.0071.
Values may be sent and summed in bfloat16 or wider, within the bound.
A program may use at most 64 MiB of HBM per device.

```python
import jax
import jax.numpy as jnp
from jax import lax

INPUTS = 2048
TILE = 64
NFFT = 2048
NCHAN = 1024
TILES = 32
NPAIR = 128
FRAMES = 16
SEL = 16


def draw_channels(key, part):
    interior = jax.random.permutation(key, jnp.arange(1, NCHAN - 1, dtype=jnp.int32))[:SEL - 2]
    picked = jnp.concatenate([interior, jnp.array([0, NCHAN - 1], dtype=jnp.int32)])
    return jax.random.permutation(jax.random.fold_in(key, 7), picked)


def draw_tile_pairs(key, part):
    interior = jax.random.permutation(key, jnp.arange(1, TILES * TILES - 1, dtype=jnp.int32))[:NPAIR - 2]
    picked = jnp.concatenate([interior, jnp.array([0, TILES * TILES - 1], dtype=jnp.int32)])
    picked = jax.random.permutation(jax.random.fold_in(key, 11), picked)
    return jnp.stack([picked // TILES, picked % TILES], 1)


def block_levels(own_key, dims, cuts, low, high):
    gain = 1.0
    for position, parts in cuts:
        draws = jax.random.uniform(jax.random.fold_in(jax.random.fold_in(own_key, 6), position), (parts,), jnp.float32, low / len(cuts), high / len(cuts))
        gain = gain * jnp.repeat(jnp.exp(draws), dims[position] // parts).reshape((-1,) + (1,) * (len(dims) - 1 - position))
    return gain


def normal_values(stream_key, shape, deviation, most, cuts=(), kind=jnp.bfloat16):
    factor_of = block_levels(stream_key, shape, cuts, -0.22, 0.18) if cuts else 1.0
    drawn = jax.random.normal(stream_key, shape, jnp.float32) * deviation * factor_of
    return jnp.minimum(jnp.maximum(drawn, -most), most).astype(kind)


def setup_inputs(seed: int = 0, part: int = 0) -> dict:
    key_list = jax.random.split(jax.random.key(seed), 4)
    part_splits = jax.random.split(jax.random.fold_in(key_list[3], part), 4)
    return {
        "voltages": normal_values(part_splits[0], (INPUTS, FRAMES * NFFT), 1.0, 6.0, ((0, 8), (1, 2))),
        "channels": draw_channels(jax.random.fold_in(key_list[3], 71), part),
        "tile_pairs": draw_tile_pairs(jax.random.fold_in(key_list[3], 71), part),
    }


def dft_table(channels, length):
    samples = jnp.arange(length, dtype=jnp.int32)
    phase = channels[:, None] * samples[None, :] % length
    angle = 2.0 * jnp.pi / length * phase.astype(jnp.float32)
    window = 0.5 - 0.5 * jnp.cos(2.0 * jnp.pi / length * samples.astype(jnp.float32))
    scale = 1.0 / jnp.sqrt(jnp.float32(0.375 * length))
    table = jnp.concatenate([window * jnp.cos(angle), -window * jnp.sin(angle)], 0) * scale
    return table.astype(jnp.bfloat16)

def reference(voltages, channels, tile_pairs):
    table = dft_table(channels, NFFT)
    blocks = voltages.reshape(INPUTS // TILE, TILE * FRAMES, NFFT)

    def transform(block):
        return jnp.dot(table, block.T, preferred_element_type=jnp.float32).astype(jnp.bfloat16)
    spectra = lax.map(transform, blocks)
    spectra = spectra.reshape(INPUTS // TILE, 2, SEL, TILE, FRAMES)
    spectra = spectra.transpose(2, 1, 0, 3, 4).reshape(SEL, 2, INPUTS, FRAMES)

    def one_channel(spec):

        def one_pair(pair):
            first = lax.dynamic_slice_in_dim(spec, (pair[0] * TILE).astype(jnp.int32), TILE, 1).reshape(2 * TILE, FRAMES)
            second = lax.dynamic_slice_in_dim(spec, (pair[1] * TILE).astype(jnp.int32), TILE, 1).reshape(2 * TILE, FRAMES)
            prod = jnp.dot(first, second.T, preferred_element_type=jnp.float32)
            real = prod[:TILE, :TILE] + prod[TILE:, TILE:]
            imag = prod[:TILE, TILE:] - prod[TILE:, :TILE]
            return (jnp.concatenate([real, imag], 1) / FRAMES).astype(jnp.bfloat16)
        return lax.map(one_pair, tile_pairs)
    return lax.map(one_channel, spectra)
```

```python
import functools

import jax
import jax.numpy as jnp
from jax import lax
from jax.experimental import pallas as pl
from jax.experimental.pallas import tpu as pltpu
from jax.sharding import PartitionSpec as P

TILE = 64
NFFT = 2048
LANES = 128
SUBLANES = 8
OUT = pltpu.VMEM
UNROLL = 16
KSPLIT = 1
GROUP = 2
MAXCHUNKS = 1
MESH = pl.DeviceIdType.MESH


def cos_sin(multiplier, steps):
    phase = lax.rem(multiplier * steps, NFFT)
    angle = (2.0 * jnp.pi / NFFT) * phase.astype(jnp.float32)
    return jnp.cos(angle), jnp.sin(angle)


def fill_table(channels_ref, table):
    count = channels_ref.shape[1]
    highs = NFFT // LANES
    scale = 1.0 / jnp.sqrt(jnp.float32(0.375 * NFFT))
    square = (count, count)
    diagonal = lax.broadcasted_iota(jnp.int32, square, 0) == lax.broadcasted_iota(jnp.int32, square, 1)
    row = jnp.broadcast_to(channels_ref[...].astype(jnp.float32), square)
    channels = jnp.sum(jnp.where(diagonal, row, 0.0), axis=1, keepdims=True).astype(jnp.int32)
    low = lax.broadcasted_iota(jnp.int32, (count, LANES), 1)
    low_cos, low_sin = cos_sin(channels, low)
    high_cos, high_sin = cos_sin(channels, LANES * low)
    win_low = lax.broadcasted_iota(jnp.int32, (8, LANES), 1)
    win_cos, win_sin = cos_sin(1, win_low)
    win_high_cos, win_high_sin = cos_sin(1, LANES * win_low)
    for high in range(highs):
        columns = slice(high * LANES, (high + 1) * LANES)
        wc, ws = win_high_cos[:, high : high + 1], win_high_sin[:, high : high + 1]
        window = (0.5 - 0.5 * (win_cos * wc - win_sin * ws)) * scale
        window = jnp.broadcast_to(window[:1], (count, LANES))
        hc, hs = high_cos[:, high : high + 1], high_sin[:, high : high + 1]
        real = window * (low_cos * hc - low_sin * hs)
        imag = -window * (low_sin * hc + low_cos * hs)
        table[:, columns] = jnp.concatenate([real, imag], 0).astype(jnp.bfloat16)


def transformed(table, block):
    half = NFFT // KSPLIT
    return sum(
        lax.dot_general(
            table[:, k : k + half],
            block[:, k : k + half],
            (((1,), (1,)), ((), ())),
            preferred_element_type=jnp.float32,
        )
        for k in range(0, NFFT, half)
    )


def transform_kernel(
    n_wide, n_tm, channels_hbm, v_hbm, pairs_hbm, out, pairs_out, channels, blocks, table, staged, send, in_sems, send_sem, recv_sem
):
    frames, in_dev, _ = blocks.shape
    chunks, count, rows, _ = send.shape
    part = frames // chunks
    group = GROUP if part % GROUP == 0 else 1
    wide, tm = lax.axis_index("wide"), lax.axis_index("tm")
    me = wide * n_tm + tm
    peers = n_wide * n_tm
    per_dev = count // peers

    fetch = pltpu.make_async_copy(channels_hbm, channels, in_sems.at[frames])
    fetch.start()
    pf = pltpu.make_async_copy(pairs_hbm, pairs_out, in_sems.at[frames + 1])
    pf.start()
    loads = [
        pltpu.make_async_copy(
            v_hbm.at[:, pl.ds(f * NFFT, NFFT)], blocks.at[f], in_sems.at[f]
        )
        for f in range(frames)
    ]
    for load in loads:
        load.start()

    def device(peer):
        return {"wide": peer // n_tm, "tm": lax.rem(peer, n_tm)}

    barrier = pltpu.get_barrier_semaphore()

    def greet(k, carry):
        peer = lax.rem(me + k, peers)
        pl.semaphore_signal(barrier, inc=1, device_id=device(peer), device_id_type=MESH)
        return carry

    lax.fori_loop(1, peers, greet, 0)

    fetch.wait()
    pf.wait()
    fill_table(channels, table)

    upper = 2 * wide // n_wide
    own_turn = upper * me + (1 - upper) * (peers - 1 - me)

    def peer_at(k):
        turn = k + (k + peers - own_turn) // peers
        return upper * turn + (1 - upper) * (peers - 1 - turn)

    def copy_to(chunk, peer):
        return pltpu.make_async_remote_copy(
            src_ref=send.at[chunk, pl.ds(peer * per_dev, per_dev)],
            dst_ref=out.at[wide, tm, chunk],
            send_sem=send_sem,
            recv_sem=recv_sem,
            device_id=device(peer),
            device_id_type=MESH,
        )

    for c in range(chunks):
        for f0 in range(c * part, (c + 1) * part, group):
            members = range(f0, f0 + group)
            for f in members:
                loads[f].wait()
            spectrum = [transformed(table, blocks.at[f]) for f in members]
            for f, values in zip(members, spectrum):
                for q in range(2):
                    staged[c, :, q * part + f - c * part, :] = values[q * count : (q + 1) * count]
        send[c] = staged[c].astype(jnp.bfloat16)

        if c == 0:
            pl.semaphore_wait(barrier, peers - 1)

        def start(k, carry):
            copy_to(c, peer_at(k)).start()
            return carry

        lax.fori_loop(0, peers - 1, start, 0, unroll=peers <= UNROLL)
        own = pltpu.make_async_copy(
            send.at[c, pl.ds(me * per_dev, per_dev)], out.at[wide, tm, c], recv_sem
        )
        own.start()

    others = send.at[:, pl.ds(0, (peers - 1) * per_dev)]
    pltpu.make_async_copy(others, others, send_sem).wait()
    pltpu.make_async_copy(send, send, recv_sem).wait()


def transform(voltages, channels, pairs, n_wide, n_tm):
    in_dev, samples = voltages.shape
    frames = samples // NFFT
    count = channels.shape[0]
    peers = n_wide * n_tm
    chunks = min(MAXCHUNKS, max(1, 2 * frames // SUBLANES))
    rows = 2 * frames // chunks
    return pl.pallas_call(
        functools.partial(transform_kernel, n_wide, n_tm),
        out_shape=(pltpu.VMEM((n_wide, n_tm, chunks, count // peers, rows, in_dev), jnp.bfloat16), pltpu.SMEM(pairs.shape, jnp.int32)),
        in_specs=[pl.BlockSpec(memory_space=pltpu.HBM)] * 3,
        out_specs=(pl.BlockSpec(memory_space=OUT), pl.BlockSpec(memory_space=pltpu.SMEM)),
        scratch_shapes=[
            pltpu.VMEM((1, count), jnp.int32),
            pltpu.VMEM((frames, in_dev, NFFT), jnp.bfloat16),
            pltpu.VMEM((2 * count, NFFT), jnp.bfloat16),
            pltpu.VMEM((chunks, count, rows, in_dev), jnp.float32),
            pltpu.VMEM((chunks, count, rows, in_dev), jnp.bfloat16),
            pltpu.SemaphoreType.DMA((frames + 2,)),
            pltpu.SemaphoreType.DMA,
            pltpu.SemaphoreType.DMA,
        ],
        compiler_params=pltpu.CompilerParams(collective_id=0, has_side_effects=True, vmem_limit_bytes=40<<20),
        name="transform",
    )(pltpu.with_memory_space_constraint(channels.reshape(1, count), pltpu.HBM), pltpu.with_memory_space_constraint(voltages, pltpu.HBM), pltpu.with_memory_space_constraint(pairs, pltpu.HBM))


def correlate_kernel(frames, chunk, pairs_ref, spectra, out, left, right, products, sems):
    groups, n_tm, chunks, rows, in_group = spectra.shape
    half = rows // 2
    npairs = out.shape[0]
    for g in range(groups):
        blocks = [spectra[g, t, c].astype(jnp.float32) for t in range(n_tm) for c in range(chunks)]
        plain = jnp.concatenate(blocks, 0)
        swapped = jnp.concatenate([x for b in blocks for x in (b[half:], -b[:half])], 0)
        left[g * in_group : (g + 1) * in_group, :] = plain.T.astype(jnp.bfloat16)
        for j in range(in_group // TILE):
            columns = slice(j * TILE, (j + 1) * TILE)
            both = jnp.concatenate([plain[:, columns], swapped[:, columns]], 1)
            right[g * (in_group // TILE) + j] = both.astype(jnp.bfloat16)

    copies = []
    for c in range(npairs // chunk):
        for p in range(c * chunk, (c + 1) * chunk):
            first = left[pl.ds(pl.multiple_of(pairs_ref[0, p] * TILE, TILE), TILE), :]
            second = right[pairs_ref[1, p]]
            sums = jnp.dot(first, second, preferred_element_type=jnp.float32)
            products[p] = (sums * (1.0 / frames)).astype(jnp.bfloat16)
        span = pl.ds(c * chunk, chunk)
        copy = pltpu.make_async_copy(products.at[span], out.at[span], sems.at[c])
        copy.start()
        copies.append(copy)
    for copy in copies:
        copy.wait()


def correlate(spectra, pairs, frames):
    groups, n_tm, chunks, rows, in_group = spectra.shape
    npairs = pairs.shape[1]
    inputs = groups * in_group
    depth = n_tm * chunks * rows
    chunk = 16 if npairs % 16 == 0 else npairs
    return pl.pallas_call(
        functools.partial(correlate_kernel, frames, chunk),
        out_shape=jax.ShapeDtypeStruct((npairs, TILE, 2 * TILE), jnp.bfloat16),
        in_specs=[
            pl.BlockSpec(memory_space=pltpu.SMEM),
            pl.BlockSpec(memory_space=pltpu.VMEM),
        ],
        out_specs=pl.BlockSpec(memory_space=pltpu.HBM),
        scratch_shapes=[
            pltpu.VMEM((inputs, depth), jnp.bfloat16),
            pltpu.VMEM((inputs // TILE, depth, 2 * TILE), jnp.bfloat16),
            pltpu.VMEM((npairs, TILE, 2 * TILE), jnp.bfloat16),
            pltpu.SemaphoreType.DMA((npairs // chunk,)),
        ],
        compiler_params=pltpu.CompilerParams(vmem_limit_bytes=40<<20),
        name="correlate",
    )(pltpu.with_memory_space_constraint(pairs, pltpu.SMEM), spectra)


def shards(voltages, channels, tile_pairs):
    n_wide = lax.axis_size("wide")
    n_tm = lax.axis_size("tm")
    in_dev = voltages.shape[0]
    frames_all = voltages.shape[1] // NFFT * n_tm
    per_dev = channels.shape[0] // (n_wide * n_tm)
    turned, pairs = transform(voltages, channels, tile_pairs.T, n_wide, n_tm)
    visibility = []
    for s in range(per_dev):
        spectra = turned[:, :, :, s]
        if in_dev % TILE:
            chunks, rows = spectra.shape[2:4]
            spectra = spectra.transpose(1, 2, 3, 0, 4).reshape(1, n_tm, chunks, rows, n_wide * in_dev)
        visibility.append(correlate(spectra, pairs, frames_all))
    return jnp.stack(visibility)


def solution(mesh):
    return jax.shard_map(
        shards,
        mesh=mesh,
        in_specs=(P("wide", ("grp", "tm")), P(), P()),
        out_specs=P(("grp", "wide", "tm"), None, None, None),
        check_vma=False,
    )
```

```python
import functools

import jax
import jax.numpy as jnp
from jax import lax
from jax.experimental import pallas as pl
from jax.experimental.pallas import tpu as pltpu
from jax.sharding import PartitionSpec as P

TILE = 64
NFFT = 2048
LANES = 128
SUBLANES = 8
OUT = pltpu.VMEM
UNROLL = 16
GROUP = 2
MXU = 256
MAXCHUNKS = 1
MESH = pl.DeviceIdType.MESH


def cos_sin(multiplier, steps):
    phase = lax.rem(multiplier * steps, NFFT)
    angle = (2.0 * jnp.pi / NFFT) * phase.astype(jnp.float32)
    return jnp.cos(angle), jnp.sin(angle)


def fill_table(channels_ref, table):
    count = channels_ref.shape[1]
    highs = NFFT // LANES
    scale = 1.0 / jnp.sqrt(jnp.float32(0.375 * NFFT))
    square = (count, count)
    diagonal = lax.broadcasted_iota(jnp.int32, square, 0) == lax.broadcasted_iota(jnp.int32, square, 1)
    row = jnp.broadcast_to(channels_ref[...].astype(jnp.float32), square)
    channels = jnp.sum(jnp.where(diagonal, row, 0.0), axis=1, keepdims=True).astype(jnp.int32)
    low = lax.broadcasted_iota(jnp.int32, (count, LANES), 1)
    low_cos, low_sin = cos_sin(channels, low)
    high_cos, high_sin = cos_sin(channels, LANES * low)
    win_low = lax.broadcasted_iota(jnp.int32, (8, LANES), 1)
    win_cos, win_sin = cos_sin(1, win_low)
    win_high_cos, win_high_sin = cos_sin(1, LANES * win_low)
    for high in range(highs):
        columns = slice(high * LANES, (high + 1) * LANES)
        wc, ws = win_high_cos[:, high : high + 1], win_high_sin[:, high : high + 1]
        window = (0.5 - 0.5 * (win_cos * wc - win_sin * ws)) * scale
        window = jnp.broadcast_to(window[:1], (count, LANES))
        hc, hs = high_cos[:, high : high + 1], high_sin[:, high : high + 1]
        real = window * (low_cos * hc - low_sin * hs)
        imag = -window * (low_sin * hc + low_cos * hs)
        table[:, columns] = jnp.concatenate([real, imag], 0).astype(jnp.bfloat16)


def transformed(table, block):
    return lax.dot_general(
        table[...], block[...], (((1,), (1,)), ((), ())), preferred_element_type=jnp.float32
    )


def transform_kernel(
    n_wide, n_tm, channels_hbm, v_hbm, pairs_hbm, out, pairs_out, channels, blocks, table, staged, send, in_sems, send_sem, recv_sem
):
    frames, in_dev, _ = blocks.shape
    chunks, count, rows, _ = send.shape
    part = frames // chunks
    group = GROUP if part % GROUP == 0 else 1
    wide, tm = lax.axis_index("wide"), lax.axis_index("tm")
    me = wide * n_tm + tm
    peers = n_wide * n_tm
    per_dev = count // peers

    fetch = pltpu.make_async_copy(channels_hbm, channels, in_sems.at[frames])
    fetch.start()
    pf = pltpu.make_async_copy(pairs_hbm, pairs_out, in_sems.at[frames + 1])
    pf.start()
    loads = [
        pltpu.make_async_copy(
            v_hbm.at[:, pl.ds(f * NFFT, NFFT)], blocks.at[f], in_sems.at[f]
        )
        for f in range(frames)
    ]
    for load in loads:
        load.start()

    def device(peer):
        return {"wide": peer // n_tm, "tm": lax.rem(peer, n_tm)}

    barrier = pltpu.get_barrier_semaphore()

    def greet(k, carry):
        peer = lax.rem(me + k, peers)
        pl.semaphore_signal(barrier, inc=1, device_id=device(peer), device_id_type=MESH)
        return carry

    lax.fori_loop(1, peers, greet, 0)

    fetch.wait()
    pf.wait()
    fill_table(channels, table)

    upper = 2 * wide // n_wide
    own_turn = upper * me + (1 - upper) * (peers - 1 - me)

    def peer_at(k):
        turn = k + (k + peers - own_turn) // peers
        return upper * turn + (1 - upper) * (peers - 1 - turn)

    def copy_to(chunk, peer):
        return pltpu.make_async_remote_copy(
            src_ref=send.at[chunk, pl.ds(peer * per_dev, per_dev)],
            dst_ref=out.at[wide, tm, chunk],
            send_sem=send_sem,
            recv_sem=recv_sem,
            device_id=device(peer),
            device_id_type=MESH,
        )

    def finish(f, values):
        c, row = f // part, f % part
        for q in range(2):
            staged[c, :, q * part + row, :] = values[q * count : (q + 1) * count]
        if row < part - 1:
            return
        send[c] = staged[c].astype(jnp.bfloat16)
        if c == 0:
            pl.semaphore_wait(barrier, peers - 1)

        def start(k, carry):
            copy_to(c, peer_at(k)).start()
            return carry

        lax.fori_loop(0, peers - 1, start, 0, unroll=peers <= UNROLL)
        pltpu.make_async_copy(
            send.at[c, pl.ds(me * per_dev, per_dev)], out.at[wide, tm, c], recv_sem
        ).start()

    if in_dev == MXU:

        def pipelined(*sums):
            def pop(f):
                return pltpu.matmul_pop(sums[f % 2]) + pltpu.matmul_pop(sums[2 + f % 2])

            for f in range(frames):
                loads[f].wait()
                for k in range(NFFT // MXU):
                    unit, slot = k % 2, k // 2 % 2
                    columns = slice(k * MXU, (k + 1) * MXU)
                    pltpu.matmul_push_rhs(blocks[f, :, columns], slot, unit, transpose=True)
                    pltpu.matmul_acc_lhs(sums[2 * unit + f % 2], table[:, columns], load_staged_rhs=slot)
                if f:
                    finish(f - 1, pop(f - 1))
            finish(frames - 1, pop(frames - 1))

        sums = [pltpu.ACC(unit)((2 * count, in_dev), jnp.float32) for unit in (0, 0, 1, 1)]
        pl.run_scoped(pipelined, *sums)
    else:
        for f0 in range(0, frames, group):
            members = range(f0, f0 + group)
            for f in members:
                loads[f].wait()
            spectrum = [transformed(table, blocks.at[f]) for f in members]
            for f, values in zip(members, spectrum):
                finish(f, values)

    others = send.at[:, pl.ds(0, (peers - 1) * per_dev)]
    pltpu.make_async_copy(others, others, send_sem).wait()
    pltpu.make_async_copy(send, send, recv_sem).wait()


def transform(voltages, channels, pairs, n_wide, n_tm):
    in_dev, samples = voltages.shape
    frames = samples // NFFT
    count = channels.shape[0]
    peers = n_wide * n_tm
    chunks = min(MAXCHUNKS, max(1, 2 * frames // SUBLANES))
    rows = 2 * frames // chunks
    return pl.pallas_call(
        functools.partial(transform_kernel, n_wide, n_tm),
        out_shape=(pltpu.VMEM((n_wide, n_tm, chunks, count // peers, rows, in_dev), jnp.bfloat16), pltpu.SMEM(pairs.shape, jnp.int32)),
        in_specs=[pl.BlockSpec(memory_space=pltpu.HBM)] * 3,
        out_specs=(pl.BlockSpec(memory_space=OUT), pl.BlockSpec(memory_space=pltpu.SMEM)),
        scratch_shapes=[
            pltpu.VMEM((1, count), jnp.int32),
            pltpu.VMEM((frames, in_dev, NFFT), jnp.bfloat16),
            pltpu.VMEM((2 * count, NFFT), jnp.bfloat16),
            pltpu.VMEM((chunks, count, rows, in_dev), jnp.float32),
            pltpu.VMEM((chunks, count, rows, in_dev), jnp.bfloat16),
            pltpu.SemaphoreType.DMA((frames + 2,)),
            pltpu.SemaphoreType.DMA,
            pltpu.SemaphoreType.DMA,
        ],
        compiler_params=pltpu.CompilerParams(collective_id=0, has_side_effects=True, vmem_limit_bytes=40<<20),
        name="transform",
    )(pltpu.with_memory_space_constraint(channels.reshape(1, count), pltpu.HBM), pltpu.with_memory_space_constraint(voltages, pltpu.HBM), pltpu.with_memory_space_constraint(pairs, pltpu.HBM))


def correlate_kernel(frames, chunk, pairs_ref, spectra, out, left, right, products, sems):
    groups, n_tm, chunks, rows, in_group = spectra.shape
    half = rows // 2
    npairs = out.shape[0]
    for g in range(groups):
        blocks = [spectra[g, t, c].astype(jnp.float32) for t in range(n_tm) for c in range(chunks)]
        plain = jnp.concatenate(blocks, 0)
        swapped = jnp.concatenate([x for b in blocks for x in (b[half:], -b[:half])], 0)
        left[g * in_group : (g + 1) * in_group, :] = plain.T.astype(jnp.bfloat16)
        for j in range(in_group // TILE):
            columns = slice(j * TILE, (j + 1) * TILE)
            both = jnp.concatenate([plain[:, columns], swapped[:, columns]], 1)
            right[g * (in_group // TILE) + j] = both.astype(jnp.bfloat16)

    copies = []
    for c in range(npairs // chunk):
        for p in range(c * chunk, (c + 1) * chunk):
            first = left[pl.ds(pl.multiple_of(pairs_ref[0, p] * TILE, TILE), TILE), :]
            second = right[pairs_ref[1, p]]
            sums = jnp.dot(first, second, preferred_element_type=jnp.float32)
            products[p] = (sums * (1.0 / frames)).astype(jnp.bfloat16)
        span = pl.ds(c * chunk, chunk)
        copy = pltpu.make_async_copy(products.at[span], out.at[span], sems.at[c])
        copy.start()
        copies.append(copy)
    for copy in copies:
        copy.wait()


def correlate(spectra, pairs, frames):
    groups, n_tm, chunks, rows, in_group = spectra.shape
    npairs = pairs.shape[1]
    inputs = groups * in_group
    depth = n_tm * chunks * rows
    chunk = 16 if npairs % 16 == 0 else npairs
    return pl.pallas_call(
        functools.partial(correlate_kernel, frames, chunk),
        out_shape=jax.ShapeDtypeStruct((npairs, TILE, 2 * TILE), jnp.bfloat16),
        in_specs=[
            pl.BlockSpec(memory_space=pltpu.SMEM),
            pl.BlockSpec(memory_space=pltpu.VMEM),
        ],
        out_specs=pl.BlockSpec(memory_space=pltpu.HBM),
        scratch_shapes=[
            pltpu.VMEM((inputs, depth), jnp.bfloat16),
            pltpu.VMEM((inputs // TILE, depth, 2 * TILE), jnp.bfloat16),
            pltpu.VMEM((npairs, TILE, 2 * TILE), jnp.bfloat16),
            pltpu.SemaphoreType.DMA((npairs // chunk,)),
        ],
        compiler_params=pltpu.CompilerParams(vmem_limit_bytes=40<<20),
        name="correlate",
    )(pltpu.with_memory_space_constraint(pairs, pltpu.SMEM), spectra)


def shards(voltages, channels, tile_pairs):
    n_wide = lax.axis_size("wide")
    n_tm = lax.axis_size("tm")
    in_dev = voltages.shape[0]
    frames_all = voltages.shape[1] // NFFT * n_tm
    per_dev = channels.shape[0] // (n_wide * n_tm)
    turned, pairs = transform(voltages, channels, tile_pairs.T, n_wide, n_tm)
    visibility = []
    for s in range(per_dev):
        spectra = turned[:, :, :, s]
        if in_dev % TILE:
            chunks, rows = spectra.shape[2:4]
            spectra = spectra.transpose(1, 2, 3, 0, 4).reshape(1, n_tm, chunks, rows, n_wide * in_dev)
        visibility.append(correlate(spectra, pairs, frames_all))
    return jnp.stack(visibility)


def solution(mesh):
    mapped = jax.shard_map(
        shards,
        mesh=mesh,
        in_specs=(P("wide", ("grp", "tm")), P(), P()),
        out_specs=P(("grp", "wide", "tm"), None, None, None),
        check_vma=False,
    )

    def traced(*args):
        with jax.sharding.use_abstract_mesh(mesh.abstract_mesh):
            return mapped(*args)

    return traced
```

```python
import functools

import jax
import jax.numpy as jnp
from jax import lax
from jax.experimental import pallas as pl
from jax.experimental.pallas import tpu as pltpu
from jax.sharding import PartitionSpec as P

TILE = 64
NFFT = 2048
LANES = 128
SUBLANES = 8
UNROLL = 16
GROUP = 2
MXU = 256
MAXCHUNKS = 1
LAST = 1
POP_AT = 7
CHUNK = 16
VMEM_LIMIT = 40 << 20
MESH = pl.DeviceIdType.MESH


def cos_sin(multiplier, steps):
    phase = lax.rem(multiplier * steps, NFFT)
    angle = (2.0 * jnp.pi / NFFT) * phase.astype(jnp.float32)
    return jnp.cos(angle), jnp.sin(angle)


def fill_table(channels_ref, table):
    count = channels_ref.shape[1]
    highs = NFFT // LANES
    scale = 1.0 / jnp.sqrt(jnp.float32(0.375 * NFFT))
    square = (count, count)
    diagonal = lax.broadcasted_iota(jnp.int32, square, 0) == lax.broadcasted_iota(jnp.int32, square, 1)
    row = jnp.broadcast_to(channels_ref[...].astype(jnp.float32), square)
    channels = jnp.sum(jnp.where(diagonal, row, 0.0), axis=1, keepdims=True).astype(jnp.int32)
    low = lax.broadcasted_iota(jnp.int32, (count, LANES), 1)
    low_cos, low_sin = cos_sin(channels, low)
    high_cos, high_sin = cos_sin(channels, LANES * low)
    win_low = lax.broadcasted_iota(jnp.int32, (8, LANES), 1)
    win_cos, win_sin = cos_sin(1, win_low)
    win_high_cos, win_high_sin = cos_sin(1, LANES * win_low)
    for high in range(highs):
        columns = slice(high * LANES, (high + 1) * LANES)
        wc, ws = win_high_cos[:, high : high + 1], win_high_sin[:, high : high + 1]
        window = (0.5 - 0.5 * (win_cos * wc - win_sin * ws)) * scale
        window = jnp.broadcast_to(window[:1], (count, LANES))
        hc, hs = high_cos[:, high : high + 1], high_sin[:, high : high + 1]
        real = window * (low_cos * hc - low_sin * hs)
        imag = -window * (low_sin * hc + low_cos * hs)
        table[:, columns] = jnp.concatenate([real, imag], 0).astype(jnp.bfloat16)


def transformed(table, block):
    return lax.dot_general(
        table[...], block[...], (((1,), (1,)), ((), ())), preferred_element_type=jnp.float32
    )


def transform_kernel(n_wide, n_tm, prepared, channels_hbm, v_hbm, pairs_hbm, *refs):
    if prepared:
        left, right, pairs, turned, *scratch = refs
    else:
        turned, pairs, *scratch = refs
    channels, blocks, table, staged, send, sems, send_sem, recv_sems = scratch
    frames, in_dev, _ = blocks.shape
    chunks, count, rows, _ = send.shape
    part = frames // chunks
    group = GROUP if part % GROUP == 0 else 1
    wide, tm = lax.axis_index("wide"), lax.axis_index("tm")
    me = wide * n_tm + tm
    peers = n_wide * n_tm
    per_dev = count // peers

    fetch = pltpu.make_async_copy(channels_hbm, channels, sems.at[len(load_pieces(frames))])
    fetch.start()
    loads = []
    for piece, (f, start, width) in enumerate(load_pieces(frames)):
        columns = pl.ds(f * NFFT + start, width)
        load = pltpu.make_async_copy(
            v_hbm.at[:, columns], blocks.at[f, :, pl.ds(start, width)], sems.at[piece]
        )
        load.start()
        loads.append((f, start, load))
    fetch_pairs = pltpu.make_async_copy(pairs_hbm, pairs, sems.at[len(load_pieces(frames))+1])
    fetch_pairs.start()

    def wait_load(frame, low, high):
        for f, start, load in loads:
            if f == frame and low <= start < high:
                load.wait()

    def device(peer):
        return {"wide": peer // n_tm, "tm": lax.rem(peer, n_tm)}

    barrier = pltpu.get_barrier_semaphore()

    def greet(k, carry):
        peer = lax.rem(me + k, peers)
        pl.semaphore_signal(barrier, inc=1, device_id=device(peer), device_id_type=MESH)
        return carry

    lax.fori_loop(1, peers, greet, 0)

    fetch.wait()
    fill_table(channels, table)

    upper = 2 * wide // n_wide
    own_turn = upper * me + (1 - upper) * (peers - 1 - me)

    def peer_at(k):
        turn = k + (k + peers - own_turn) // peers
        return upper * turn + (1 - upper) * (peers - 1 - turn)

    def round_for(c, peer):
        span = pl.ds(peer * per_dev, per_dev)
        send[c, span] = staged[c, span].astype(jnp.bfloat16)
        return send.at[c, span]

    def finish(f, values):
        c, row = f // part, f % part
        for q in range(2):
            staged[c, :, q * part + row, :] = values[q * count : (q + 1) * count]
        if row < part - 1:
            return
        if c == 0:
            pl.semaphore_wait(barrier, peers - 1)

        def start(k, carry):
            peer = peer_at(k)
            pltpu.make_async_remote_copy(
                src_ref=round_for(c, peer),
                dst_ref=turned.at[wide, tm, c],
                send_sem=send_sem,
                recv_sem=recv_sems.at[wide],
                device_id=device(peer),
                device_id_type=MESH,
            ).start()
            return carry

        lax.fori_loop(0, peers - 1, start, 0, unroll=peers <= UNROLL)
        pltpu.make_async_copy(round_for(c, me), turned.at[wide, tm, c], recv_sems.at[wide]).start()

    if in_dev == MXU:

        def pipelined(*sums):
            def pop(f):
                return pltpu.matmul_pop(sums[f % 2]) + pltpu.matmul_pop(sums[2 + f % 2])

            for f in range(frames):
                for k in range(NFFT // MXU):
                    wait_load(f, k * MXU, (k + 1) * MXU)
                    unit, slot = k % 2, k // 2 % 2
                    columns = slice(k * MXU, (k + 1) * MXU)
                    pltpu.matmul_push_rhs(blocks[f, :, columns], slot, unit, transpose=True)
                    pltpu.matmul_acc_lhs(sums[2 * unit + f % 2], table[:, columns], load_staged_rhs=slot)
                    if f and k == POP_AT:
                        finish(f - 1, pop(f - 1))
            finish(frames - 1, pop(frames - 1))

        sums = [pltpu.ACC(unit)((2 * count, in_dev), jnp.float32) for unit in (0, 0, 1, 1)]
        pl.run_scoped(pipelined, *sums)
    else:
        for f0 in range(0, frames, group):
            members = range(f0, f0 + group)
            for f in members:
                wait_load(f, 0, NFFT)
            spectrum = [transformed(table, blocks.at[f]) for f in members]
            for f, values in zip(members, spectrum):
                finish(f, values)

    def arrive(k, carry):
        g = upper * (n_wide - 1 - k) + (1 - upper) * k
        pltpu.make_async_copy(turned.at[g], turned.at[g], recv_sems.at[g]).wait()
        if prepared:
            prepare([turned[g, t, c, 0] for t in range(n_tm) for c in range(chunks)], left, right, g)
        return carry

    fetch_pairs.wait()
    lax.fori_loop(0, n_wide, arrive, 0, unroll=n_wide <= UNROLL)
    others = send.at[:, pl.ds(0, (peers - 1) * per_dev)]
    pltpu.make_async_copy(others, others, send_sem).wait()


def load_pieces(frames):
    whole = [(f, 0, NFFT) for f in range(frames - 1)]
    return whole + [(frames - 1, k, NFFT // LAST) for k in range(0, NFFT, NFFT // LAST)]


def prepare(blocks, left, right, g):
    rows, in_group = blocks[0].shape
    half = rows // 2
    blocks = [block.astype(jnp.float32) for block in blocks]
    plain = jnp.concatenate(blocks, 0)
    swapped = jnp.concatenate([x for b in blocks for x in (b[half:], -b[:half])], 0)
    span = pl.ds(pl.multiple_of(g * in_group, in_group), in_group)
    left[span, :] = plain.T.astype(jnp.bfloat16)
    for j in range(in_group // TILE):
        columns = slice(j * TILE, (j + 1) * TILE)
        both = jnp.concatenate([plain[:, columns], swapped[:, columns]], 1)
        right[g * (in_group // TILE) + j] = both.astype(jnp.bfloat16)


def operand_shapes(inputs, depth):
    return (inputs, depth), (inputs // TILE, depth, 2 * TILE)


def transform(voltages, channels, pairs, n_wide, n_tm, prepared):
    in_dev, samples = voltages.shape
    frames = samples // NFFT
    count = channels.shape[0]
    peers = n_wide * n_tm
    chunks = min(MAXCHUNKS, max(1, 2 * frames // SUBLANES))
    rows = 2 * frames // chunks
    turned = pltpu.VMEM((n_wide, n_tm, chunks, count // peers, rows, in_dev), jnp.bfloat16)
    made = [turned]
    if prepared:
        made = [
            pltpu.VMEM(shape, jnp.bfloat16)
            for shape in operand_shapes(n_wide * in_dev, 2 * frames * n_tm)
        ]
    inputs = channels.reshape(1, count), voltages, pairs
    return pl.pallas_call(
        functools.partial(transform_kernel, n_wide, n_tm, prepared),
        out_shape=(*made, pltpu.SMEM(pairs.shape, jnp.int32)),
        in_specs=[pl.BlockSpec(memory_space=pltpu.HBM)] * 3,
        out_specs=(
            *[pl.BlockSpec(memory_space=pltpu.VMEM)] * len(made),
            pl.BlockSpec(memory_space=pltpu.SMEM),
        ),
        scratch_shapes=[
            *([turned] if prepared else []),
            pltpu.VMEM((1, count), jnp.int32),
            pltpu.VMEM((frames, in_dev, NFFT), jnp.bfloat16),
            pltpu.VMEM((2 * count, NFFT), jnp.bfloat16),
            pltpu.VMEM((chunks, count, rows, in_dev), jnp.float32),
            pltpu.VMEM((chunks, count, rows, in_dev), jnp.bfloat16),
            pltpu.SemaphoreType.DMA((len(load_pieces(frames)) + 2 + 0,)),
            pltpu.SemaphoreType.DMA,
            pltpu.SemaphoreType.DMA((n_wide,)),
        ],
        compiler_params=pltpu.CompilerParams(
            collective_id=0, has_side_effects=True, vmem_limit_bytes=VMEM_LIMIT
        ),
        name="transform",
    )(*[pltpu.with_memory_space_constraint(x, pltpu.HBM) for x in inputs])


def correlate_kernel(frames, chunk, prepared, pairs_ref, *refs):
    if prepared:
        left, right, out, products, sems = refs
    else:
        spectra, out, products, sems, left, right = refs
        groups, n_tm, chunks, _, _ = spectra.shape
        for g in range(groups):
            prepare([spectra[g, t, c] for t in range(n_tm) for c in range(chunks)], left, right, g)
    npairs = out.shape[0]

    copies = []
    for c in range(npairs // chunk):
        for p in range(c * chunk, (c + 1) * chunk):
            first = left[pl.ds(pl.multiple_of(pairs_ref[0, p] * TILE, TILE), TILE), :]
            second = right[pairs_ref[1, p]]
            sums = jnp.dot(first, second, preferred_element_type=jnp.float32)
            products[p] = (sums * (1.0 / frames)).astype(jnp.bfloat16)
        span = pl.ds(c * chunk, chunk)
        copy = pltpu.make_async_copy(products.at[span], out.at[span], sems.at[c])
        copy.start()
        copies.append(copy)
    for copy in copies:
        copy.wait()


def correlate(operands, pairs, frames, prepared):
    npairs = pairs.shape[1]
    chunk = CHUNK if npairs % CHUNK == 0 else npairs
    scratch = [
        pltpu.VMEM((npairs, TILE, 2 * TILE), jnp.bfloat16),
        pltpu.SemaphoreType.DMA((npairs // chunk,)),
    ]
    if not prepared:
        groups, n_tm, chunks, rows, in_group = operands[0].shape
        shapes = operand_shapes(groups * in_group, n_tm * chunks * rows)
        scratch += [pltpu.VMEM(shape, jnp.bfloat16) for shape in shapes]
    return pl.pallas_call(
        functools.partial(correlate_kernel, frames, chunk, prepared),
        out_shape=jax.ShapeDtypeStruct((npairs, TILE, 2 * TILE), jnp.bfloat16),
        in_specs=[
            pl.BlockSpec(memory_space=pltpu.SMEM),
            *[pl.BlockSpec(memory_space=pltpu.VMEM)] * len(operands),
        ],
        out_specs=pl.BlockSpec(memory_space=pltpu.HBM),
        scratch_shapes=scratch,
        compiler_params=pltpu.CompilerParams(vmem_limit_bytes=VMEM_LIMIT),
        name="correlate",
    )(pltpu.with_memory_space_constraint(pairs, pltpu.SMEM), *operands)


def shards(voltages, channels, tile_pairs):
    n_wide = lax.axis_size("wide")
    n_tm = lax.axis_size("tm")
    in_dev = voltages.shape[0]
    frames_all = voltages.shape[1] // NFFT * n_tm
    per_dev = channels.shape[0] // (n_wide * n_tm)
    prepared = per_dev == 1 and in_dev % LANES == 0
    *made, pairs = transform(voltages, channels, tile_pairs.T, n_wide, n_tm, prepared)
    if prepared:
        return correlate(made, pairs, frames_all, True)[None]
    visibility = []
    for s in range(per_dev):
        spectra = made[0][:, :, :, s]
        if in_dev % TILE:
            chunks, rows = spectra.shape[2:4]
            spectra = spectra.transpose(1, 2, 3, 0, 4).reshape(1, n_tm, chunks, rows, n_wide * in_dev)
        visibility.append(correlate([spectra], pairs, frames_all, False))
    return jnp.stack(visibility)


def solution(mesh):
    mapped = jax.shard_map(
        shards,
        mesh=mesh,
        in_specs=(P("wide", ("grp", "tm")), P(), P()),
        out_specs=P(("grp", "wide", "tm"), None, None, None),
        check_vma=False,
    )

    def traced(*args):
        with jax.sharding.use_abstract_mesh(mesh.abstract_mesh):
            return mapped(*args)

    return traced
```

```python
import functools

import jax
import jax.numpy as jnp
from jax import lax
from jax.experimental import pallas as pl
from jax.experimental.pallas import tpu as pltpu
from jax.sharding import PartitionSpec as P

TILE = 64
NFFT = 2048
LANES = 128
SUBLANES = 8
UNROLL = 16
GROUP = 2
MXU = 256
MAXCHUNKS = 1
LAST = 1
POP_AT = 7
CHUNK = 16
VMEM_LIMIT = 40 << 20
MESH = pl.DeviceIdType.MESH


def cos_sin(multiplier, steps):
    phase = lax.rem(multiplier * steps, NFFT)
    angle = (2.0 * jnp.pi / NFFT) * phase.astype(jnp.float32)
    return jnp.cos(angle), jnp.sin(angle)


def fill_table(channels_ref, table):
    count = channels_ref.shape[1]
    highs = NFFT // LANES
    scale = 1.0 / jnp.sqrt(jnp.float32(0.375 * NFFT))
    square = (count, count)
    diagonal = lax.broadcasted_iota(jnp.int32, square, 0) == lax.broadcasted_iota(jnp.int32, square, 1)
    row = jnp.broadcast_to(channels_ref[...].astype(jnp.float32), square)
    channels = jnp.sum(jnp.where(diagonal, row, 0.0), axis=1, keepdims=True).astype(jnp.int32)
    low = lax.broadcasted_iota(jnp.int32, (count, LANES), 1)
    low_cos, low_sin = cos_sin(channels, low)
    high_cos, high_sin = cos_sin(channels, LANES * low)
    win_low = lax.broadcasted_iota(jnp.int32, (8, LANES), 1)
    win_cos, win_sin = cos_sin(1, win_low)
    win_high_cos, win_high_sin = cos_sin(1, LANES * win_low)
    for high in range(highs):
        columns = slice(high * LANES, (high + 1) * LANES)
        wc, ws = win_high_cos[:, high : high + 1], win_high_sin[:, high : high + 1]
        window = (0.5 - 0.5 * (win_cos * wc - win_sin * ws)) * scale
        window = jnp.broadcast_to(window[:1], (count, LANES))
        hc, hs = high_cos[:, high : high + 1], high_sin[:, high : high + 1]
        real = window * (low_cos * hc - low_sin * hs)
        imag = -window * (low_sin * hc + low_cos * hs)
        table[:, columns] = jnp.concatenate([real, imag], 0).astype(jnp.bfloat16)


def transformed(table, block):
    return lax.dot_general(
        table[...], block[...], (((1,), (1,)), ((), ())), preferred_element_type=jnp.float32
    )


def transform_kernel(n_wide, n_tm, prepared, channels_hbm, v_hbm, pairs_hbm, *refs):
    if prepared:
        left, right, pairs, turned, *scratch = refs
    else:
        turned, pairs, *scratch = refs
    channels, blocks, table, staged, send, sems, send_sem, recv_sems = scratch
    frames, in_dev, _ = blocks.shape
    chunks, count, rows, _ = send.shape
    part = frames // chunks
    group = GROUP if part % GROUP == 0 else 1
    wide, tm = lax.axis_index("wide"), lax.axis_index("tm")
    me = wide * n_tm + tm
    peers = n_wide * n_tm
    per_dev = count // peers

    fetch = pltpu.make_async_copy(channels_hbm, channels, sems.at[len(load_pieces(frames))])
    fetch.start()
    loads = []
    for piece, (f, start, width) in enumerate(load_pieces(frames)):
        columns = pl.ds(f * NFFT + start, width)
        load = pltpu.make_async_copy(
            v_hbm.at[:, columns], blocks.at[f, :, pl.ds(start, width)], sems.at[piece]
        )
        load.start()
        loads.append((f, start, load))
    fetch_pairs = pltpu.make_async_copy(pairs_hbm, pairs, sems.at[len(load_pieces(frames))+1])
    fetch_pairs.start()

    def wait_load(frame, low, high):
        for f, start, load in loads:
            if f == frame and low <= start < high:
                load.wait()

    def device(peer):
        return {"wide": peer // n_tm, "tm": lax.rem(peer, n_tm)}

    barrier = pltpu.get_barrier_semaphore()

    def greet(k, carry):
        peer = lax.rem(me + k, peers)
        pl.semaphore_signal(barrier, inc=1, device_id=device(peer), device_id_type=MESH)
        return carry

    lax.fori_loop(1, peers, greet, 0)

    fetch.wait()
    fill_table(channels, table)

    upper = 2 * wide // n_wide
    own_turn = upper * me + (1 - upper) * (peers - 1 - me)

    def peer_at(k):
        turn = k + (k + peers - own_turn) // peers
        return upper * turn + (1 - upper) * (peers - 1 - turn)

    def round_for(c, peer):
        span = pl.ds(peer * per_dev, per_dev)
        send[c, span] = staged[c, span].astype(jnp.bfloat16)
        return send.at[c, span]

    def finish(f, values):
        c, row = f // part, f % part
        for q in range(2):
            staged[c, :, q * part + row, :] = values[q * count : (q + 1) * count]
        if row < part - 1:
            return
        if c == 0:
            pl.semaphore_wait(barrier, peers - 1)

        def start(k, carry):
            peer = peer_at(k)
            pltpu.make_async_remote_copy(
                src_ref=round_for(c, peer),
                dst_ref=turned.at[wide, tm, c],
                send_sem=send_sem,
                recv_sem=recv_sems.at[wide],
                device_id=device(peer),
                device_id_type=MESH,
            ).start()
            return carry

        lax.fori_loop(0, peers - 1, start, 0, unroll=peers <= UNROLL)
        pltpu.make_async_copy(round_for(c, me), turned.at[wide, tm, c], recv_sems.at[wide]).start()

    if in_dev == MXU:

        def pipelined(*sums):
            def pop(f):
                return pltpu.matmul_pop(sums[f % 2]) + pltpu.matmul_pop(sums[2 + f % 2])

            for f in range(frames):
                for k in range(NFFT // MXU):
                    wait_load(f, k * MXU, (k + 1) * MXU)
                    unit, slot = k % 2, k // 2 % 2
                    columns = slice(k * MXU, (k + 1) * MXU)
                    pltpu.matmul_push_rhs(blocks[f, :, columns], slot, unit, transpose=True)
                    pltpu.matmul_acc_lhs(sums[2 * unit + f % 2], table[:, columns], load_staged_rhs=slot)
                    if f and k == POP_AT:
                        finish(f - 1, pop(f - 1))
            finish(frames - 1, pop(frames - 1))

        sums = [pltpu.ACC(unit)((2 * count, in_dev), jnp.float32) for unit in (0, 0, 1, 1)]
        pl.run_scoped(pipelined, *sums)
    else:
        for f0 in range(0, frames, group):
            members = range(f0, f0 + group)
            for f in members:
                wait_load(f, 0, NFFT)
            spectrum = [transformed(table, blocks.at[f]) for f in members]
            for f, values in zip(members, spectrum):
                finish(f, values)

    fetch_pairs.wait()
    others = send.at[:, pl.ds(0, (peers - 1) * per_dev)]
    pltpu.make_async_copy(others, others, send_sem).wait()
    batch = 2 if n_wide % 2 == 0 else 1

    def arrive(step, carry):
        places = [upper * (n_wide - 1 - k) + (1 - upper) * k for k in (step * batch + i for i in range(batch))]
        for g in places:
            pltpu.make_async_copy(turned.at[g], turned.at[g], recv_sems.at[g]).wait()
        if prepared:
            for g in places:
                prepare([turned[g, t, c, 0] for t in range(n_tm) for c in range(chunks)], left, right, g)
        return carry

    lax.fori_loop(0, n_wide // batch, arrive, 0, unroll=n_wide <= UNROLL)


def load_pieces(frames):
    whole = [(f, 0, NFFT) for f in range(frames - 1)]
    return whole + [(frames - 1, k, NFFT // LAST) for k in range(0, NFFT, NFFT // LAST)]


def prepare(blocks, left, right, g):
    rows, in_group = blocks[0].shape
    half = rows // 2
    plain = jnp.concatenate(blocks, 0)
    swapped = jnp.concatenate([x for b in blocks for x in (b[half:], -b[:half])], 0)
    span = pl.ds(pl.multiple_of(g * in_group, in_group), in_group)
    left[span, :] = plain.T
    for j in range(in_group // TILE):
        columns = slice(j * TILE, (j + 1) * TILE)
        both = jnp.concatenate([plain[:, columns], swapped[:, columns]], 1)
        right[g * (in_group // TILE) + j] = both


def operand_shapes(inputs, depth):
    return (inputs, depth), (inputs // TILE, depth, 2 * TILE)


def transform(voltages, channels, pairs, n_wide, n_tm, prepared):
    in_dev, samples = voltages.shape
    frames = samples // NFFT
    count = channels.shape[0]
    peers = n_wide * n_tm
    chunks = min(MAXCHUNKS, max(1, 2 * frames // SUBLANES))
    rows = 2 * frames // chunks
    turned = pltpu.VMEM((n_wide, n_tm, chunks, count // peers, rows, in_dev), jnp.bfloat16)
    made = [turned]
    if prepared:
        made = [
            pltpu.VMEM(shape, jnp.bfloat16)
            for shape in operand_shapes(n_wide * in_dev, 2 * frames * n_tm)
        ]
    inputs = channels.reshape(1, count), voltages, pairs
    return pl.pallas_call(
        functools.partial(transform_kernel, n_wide, n_tm, prepared),
        out_shape=(*made, pltpu.SMEM(pairs.shape, jnp.int32)),
        in_specs=[pl.BlockSpec(memory_space=pltpu.HBM)] * 3,
        out_specs=(
            *[pl.BlockSpec(memory_space=pltpu.VMEM)] * len(made),
            pl.BlockSpec(memory_space=pltpu.SMEM),
        ),
        scratch_shapes=[
            *([turned] if prepared else []),
            pltpu.VMEM((1, count), jnp.int32),
            pltpu.VMEM((frames, in_dev, NFFT), jnp.bfloat16),
            pltpu.VMEM((2 * count, NFFT), jnp.bfloat16),
            pltpu.VMEM((chunks, count, rows, in_dev), jnp.float32),
            pltpu.VMEM((chunks, count, rows, in_dev), jnp.bfloat16),
            pltpu.SemaphoreType.DMA((len(load_pieces(frames)) + 2 + 0,)),
            pltpu.SemaphoreType.DMA,
            pltpu.SemaphoreType.DMA((n_wide,)),
        ],
        compiler_params=pltpu.CompilerParams(
            collective_id=0, has_side_effects=True, vmem_limit_bytes=VMEM_LIMIT
        ),
        name="transform",
    )(*[pltpu.with_memory_space_constraint(x, pltpu.HBM) for x in inputs])


def correlate_kernel(frames, prepared, pairs_ref, *refs):
    if prepared:
        left, right, out, products, sem = refs
    else:
        spectra, out, products, sem, left, right = refs
        groups, n_tm, parts, _, _ = spectra.shape
        for g in range(groups):
            prepare([spectra[g, t, c] for t in range(n_tm) for c in range(parts)], left, right, g)
    npairs = out.shape[0]
    edges = [*range(0, npairs, CHUNK), npairs]
    chunks = zip(edges[:-1], edges[1:])

    for start, stop in chunks:
        for p in range(start, stop):
            first = left[pl.ds(pl.multiple_of(pairs_ref[0, p] * TILE, TILE), TILE), :]
            second = right[pairs_ref[1, p]]
            sums = jnp.dot(first, second, preferred_element_type=jnp.float32)
            products[p] = (sums * (1.0 / frames)).astype(jnp.bfloat16)
        span = pl.ds(start, stop - start)
        pltpu.make_async_copy(products.at[span], out.at[span], sem).start()
    pltpu.make_async_copy(products, out, sem).wait()


def correlate(operands, pairs, frames, prepared):
    npairs = pairs.shape[1]
    scratch = [
        pltpu.VMEM((npairs, TILE, 2 * TILE), jnp.bfloat16),
        pltpu.SemaphoreType.DMA,
    ]
    if not prepared:
        groups, n_tm, chunks, rows, in_group = operands[0].shape
        shapes = operand_shapes(groups * in_group, n_tm * chunks * rows)
        scratch += [pltpu.VMEM(shape, jnp.bfloat16) for shape in shapes]
    return pl.pallas_call(
        functools.partial(correlate_kernel, frames, prepared),
        out_shape=jax.ShapeDtypeStruct((npairs, TILE, 2 * TILE), jnp.bfloat16),
        in_specs=[
            pl.BlockSpec(memory_space=pltpu.SMEM),
            *[pl.BlockSpec(memory_space=pltpu.VMEM)] * len(operands),
        ],
        out_specs=pl.BlockSpec(memory_space=pltpu.HBM),
        scratch_shapes=scratch,
        compiler_params=pltpu.CompilerParams(vmem_limit_bytes=VMEM_LIMIT),
        name="correlate",
    )(pltpu.with_memory_space_constraint(pairs, pltpu.SMEM), *operands)


def shards(voltages, channels, tile_pairs):
    n_wide = lax.axis_size("wide")
    n_tm = lax.axis_size("tm")
    in_dev = voltages.shape[0]
    frames_all = voltages.shape[1] // NFFT * n_tm
    per_dev = channels.shape[0] // (n_wide * n_tm)
    prepared = per_dev == 1 and in_dev % LANES == 0
    *made, pairs = transform(voltages, channels, tile_pairs.T, n_wide, n_tm, prepared)
    if prepared:
        return correlate(made, pairs, frames_all, True)[None]
    visibility = []
    for s in range(per_dev):
        spectra = made[0][:, :, :, s]
        if in_dev % TILE:
            chunks, rows = spectra.shape[2:4]
            spectra = spectra.transpose(1, 2, 3, 0, 4).reshape(1, n_tm, chunks, rows, n_wide * in_dev)
        visibility.append(correlate([spectra], pairs, frames_all, False))
    return jnp.stack(visibility)


def solution(mesh):
    mapped = jax.shard_map(
        shards,
        mesh=mesh,
        in_specs=(P("wide", ("grp", "tm")), P(), P()),
        out_specs=P(("grp", "wide", "tm"), None, None, None),
        check_vma=False,
    )

    def traced(*args):
        with jax.sharding.use_abstract_mesh(mesh.abstract_mesh):
            return mapped(*args)

    return traced
```

```python
import functools

import jax
import jax.numpy as jnp
from jax import lax
from jax.experimental import pallas as pl
from jax.experimental.pallas import tpu as pltpu
from jax.sharding import PartitionSpec as P

TILE = 64
NFFT = 2048
LANES = 128
SUBLANES = 8
UNROLL = 16
GROUP = 2
MXU = 256
MAXCHUNKS = 1
CHUNK = 8
LAG = 4
VMEM_LIMIT = 40 << 20
MESH = pl.DeviceIdType.MESH


def cos_sin(multiplier, steps):
    phase = lax.rem(multiplier * steps, NFFT)
    angle = (2.0 * jnp.pi / NFFT) * phase.astype(jnp.float32)
    return jnp.cos(angle), jnp.sin(angle)


def fill_table(channels_ref, table):
    count = channels_ref.shape[1]
    highs = NFFT // LANES
    scale = 1.0 / jnp.sqrt(jnp.float32(0.375 * NFFT))
    square = (count, count)
    diagonal = lax.broadcasted_iota(jnp.int32, square, 0) == lax.broadcasted_iota(jnp.int32, square, 1)
    row = jnp.broadcast_to(channels_ref[...].astype(jnp.float32), square)
    channels = jnp.sum(jnp.where(diagonal, row, 0.0), axis=1, keepdims=True).astype(jnp.int32)
    low = lax.broadcasted_iota(jnp.int32, (count, LANES), 1)
    low_cos, low_sin = cos_sin(channels, low)
    high_cos, high_sin = cos_sin(channels, LANES * low)
    win_low = lax.broadcasted_iota(jnp.int32, (8, LANES), 1)
    win_cos, win_sin = cos_sin(1, win_low)
    win_high_cos, win_high_sin = cos_sin(1, LANES * win_low)
    for high in range(highs):
        columns = slice(high * LANES, (high + 1) * LANES)
        wc, ws = win_high_cos[:, high : high + 1], win_high_sin[:, high : high + 1]
        window = (0.5 - 0.5 * (win_cos * wc - win_sin * ws)) * scale
        window = jnp.broadcast_to(window[:1], (count, LANES))
        hc, hs = high_cos[:, high : high + 1], high_sin[:, high : high + 1]
        real = window * (low_cos * hc - low_sin * hs)
        imag = -window * (low_sin * hc + low_cos * hs)
        table[:, columns] = jnp.concatenate([real, imag], 0).astype(jnp.bfloat16)


def transformed(table, block):
    return lax.dot_general(
        table[...], block[...], (((1,), (1,)), ((), ())), preferred_element_type=jnp.float32
    )


def transform_kernel(n_wide, n_tm, prepared, channels_hbm, v_hbm, pairs_hbm, *refs):
    if prepared:
        left, right, pairs, turned, *scratch = refs
    else:
        turned, pairs, *scratch = refs
    channels, blocks, table, staged, send, sems = scratch
    frames, in_dev, _ = blocks.shape
    chunks, count, rows, _ = send.shape
    part = frames // chunks
    group = GROUP if part % GROUP == 0 else 1
    wide, tm = lax.axis_index("wide"), lax.axis_index("tm")
    me = wide * n_tm + tm
    peers = n_wide * n_tm
    per_dev = count // peers
    batch = batch_of(n_wide)

    def arrived(stage):
        return sems.at[frames + 1 + stage]

    fetch = pltpu.make_async_copy(channels_hbm, channels, sems.at[frames])
    fetch.start()
    loads = [
        pltpu.make_async_copy(v_hbm.at[:, pl.ds(f * NFFT, NFFT)], blocks.at[f], sems.at[f])
        for f in range(frames)
    ]
    for load in loads:
        load.start()

    def device(peer):
        return {"wide": peer // n_tm, "tm": lax.rem(peer, n_tm)}

    barrier = pltpu.get_barrier_semaphore()

    def greet(k, carry):
        peer = lax.rem(me + k, peers)
        pl.semaphore_signal(barrier, inc=1, device_id=device(peer), device_id_type=MESH)
        return carry

    lax.fori_loop(1, peers, greet, 0)

    fetch.wait()
    fetch_pairs = pltpu.make_async_copy(pairs_hbm, pairs, sems.at[frames])
    fetch_pairs.start()
    fill_table(channels, table)

    upper = 2 * wide // n_wide
    own_turn = upper * me + (1 - upper) * (peers - 1 - me)

    def peer_at(k):
        turn = k + (k + peers - own_turn) // peers
        return upper * turn + (1 - upper) * (peers - 1 - turn)

    def round_for(c, peer):
        span = pl.ds(peer * per_dev, per_dev)
        send[c, span] = staged[c, span].astype(jnp.bfloat16)
        return send.at[c, span]

    def finish(f, values):
        c, row = f // part, f % part
        for q in range(2):
            staged[c, :, q * part + row, :] = values[q * count : (q + 1) * count]
        if row < part - 1:
            return
        if c == 0:
            fetch_pairs.wait()
            pl.semaphore_wait(barrier, peers - 1)

        def start(k, carry):
            peer = peer_at(k)
            pltpu.make_async_remote_copy(
                src_ref=round_for(c, peer),
                dst_ref=turned.at[wide, tm, c],
                send_sem=sems.at[frames],
                recv_sem=arrived(wide // batch),
                device_id=device(peer),
                device_id_type=MESH,
            ).start()
            return carry

        lax.fori_loop(0, peers - 1, start, 0, unroll=peers <= UNROLL)
        pltpu.make_async_copy(round_for(c, me), turned.at[wide, tm, c], arrived(wide // batch)).start()

    if in_dev == MXU:

        def pipelined(*sums):
            def pop(f):
                return pltpu.matmul_pop(sums[f % 2]) + pltpu.matmul_pop(sums[2 + f % 2])

            for f in range(frames):
                loads[f].wait()
                for k in range(NFFT // MXU):
                    unit, slot = k % 2, k // 2 % 2
                    columns = slice(k * MXU, (k + 1) * MXU)
                    pltpu.matmul_push_rhs(blocks[f, :, columns], slot, unit, transpose=True)
                    pltpu.matmul_acc_lhs(sums[2 * unit + f % 2], table[:, columns], load_staged_rhs=slot)
                if f:
                    finish(f - 1, pop(f - 1))
            finish(frames - 1, pop(frames - 1))

        sums = [pltpu.ACC(unit)((2 * count, in_dev), jnp.float32) for unit in (0, 0, 1, 1)]
        pl.run_scoped(pipelined, *sums)
    else:
        for f0 in range(0, frames, group):
            members = range(f0, f0 + group)
            for f in members:
                loads[f].wait()
            spectrum = [transformed(table, blocks.at[f]) for f in members]
            for f, values in zip(members, spectrum):
                finish(f, values)

    others = send.at[:, pl.ds(0, (peers - 1) * per_dev)]
    pltpu.make_async_copy(others, others, sems.at[frames]).wait()

    def arrive(step, carry):
        stage = upper * (n_wide // batch - 1 - step) + (1 - upper) * step
        landed = turned.at[pl.ds(stage * batch, batch)]
        pltpu.make_async_copy(landed, landed, arrived(stage)).wait()
        if prepared:
            for g in range(batch):
                g = stage * batch + g
                prepare([turned[g, t, c, 0] for t in range(n_tm) for c in range(chunks)], left, right, g)
        return carry

    lax.fori_loop(0, n_wide // batch, arrive, 0, unroll=n_wide // batch <= UNROLL)


def batch_of(n_wide):
    return 2 if n_wide % 2 == 0 else 1


def prepare(blocks, left, right, g):
    rows, in_group = blocks[0].shape
    half = rows // 2
    plain = jnp.concatenate(blocks, 0)
    swapped = jnp.concatenate([x for b in blocks for x in (b[half:], -b[:half])], 0)
    span = pl.ds(pl.multiple_of(g * in_group, in_group), in_group)
    left[span, :] = plain.T
    for j in range(in_group // TILE):
        columns = slice(j * TILE, (j + 1) * TILE)
        both = jnp.concatenate([plain[:, columns], swapped[:, columns]], 1)
        right[g * (in_group // TILE) + j] = both


def operand_shapes(inputs, depth):
    return (inputs, depth), (inputs // TILE, depth, 2 * TILE)


def transform(voltages, channels, pairs, n_wide, n_tm, prepared):
    in_dev, samples = voltages.shape
    frames = samples // NFFT
    count = channels.shape[0]
    peers = n_wide * n_tm
    chunks = min(MAXCHUNKS, max(1, 2 * frames // SUBLANES))
    rows = 2 * frames // chunks
    turned = pltpu.VMEM((n_wide, n_tm, chunks, count // peers, rows, in_dev), jnp.bfloat16)
    made = [turned]
    if prepared:
        made = [
            pltpu.VMEM(shape, jnp.bfloat16)
            for shape in operand_shapes(n_wide * in_dev, 2 * frames * n_tm)
        ]
    inputs = channels.reshape(1, count), voltages, pairs
    return pl.pallas_call(
        functools.partial(transform_kernel, n_wide, n_tm, prepared),
        out_shape=(*made, pltpu.SMEM(pairs.shape, jnp.int32)),
        in_specs=[pl.BlockSpec(memory_space=pltpu.HBM)] * 3,
        out_specs=(
            *[pl.BlockSpec(memory_space=pltpu.VMEM)] * len(made),
            pl.BlockSpec(memory_space=pltpu.SMEM),
        ),
        scratch_shapes=[
            *([turned] if prepared else []),
            pltpu.VMEM((1, count), jnp.int32),
            pltpu.VMEM((frames, in_dev, NFFT), jnp.bfloat16),
            pltpu.VMEM((2 * count, NFFT), jnp.bfloat16),
            pltpu.VMEM((chunks, count, rows, in_dev), jnp.float32),
            pltpu.VMEM((chunks, count, rows, in_dev), jnp.bfloat16),
            pltpu.SemaphoreType.DMA((frames + 1 + n_wide // batch_of(n_wide),)),
        ],
        compiler_params=pltpu.CompilerParams(
            collective_id=0, has_side_effects=True, vmem_limit_bytes=VMEM_LIMIT
        ),
        name="transform",
    )(*[pltpu.with_memory_space_constraint(x, pltpu.HBM) for x in inputs])


def correlate_kernel(frames, prepared, pairs_ref, *refs):
    if prepared:
        left, right, out, products, sem = refs
    else:
        spectra, out, products, sem, left, right = refs
        groups, n_tm, parts, _, _ = spectra.shape
        for g in range(groups):
            prepare([spectra[g, t, c] for t in range(n_tm) for c in range(parts)], left, right, g)
    npairs = out.shape[0]
    waiting = []

    def store():
        p, sums = waiting.pop(0)
        products[p] = (sums * (1.0 / frames)).astype(jnp.bfloat16)
        if (p + 1) % CHUNK == 0 or p + 1 == npairs:
            start = p // CHUNK * CHUNK
            span = pl.ds(start, p + 1 - start)
            pltpu.make_async_copy(products.at[span], out.at[span], sem).start()

    for p in range(npairs):
        first = left[pl.ds(pl.multiple_of(pairs_ref[0, p] * TILE, TILE), TILE), :]
        second = right[pairs_ref[1, p]]
        waiting.append((p, jnp.dot(first, second, preferred_element_type=jnp.float32)))
        if p >= LAG:
            store()
    while waiting:
        store()
    pltpu.make_async_copy(products, out, sem).wait()


def correlate(operands, pairs, frames, prepared):
    npairs = pairs.shape[1]
    scratch = [
        pltpu.VMEM((npairs, TILE, 2 * TILE), jnp.bfloat16),
        pltpu.SemaphoreType.DMA,
    ]
    if not prepared:
        groups, n_tm, chunks, rows, in_group = operands[0].shape
        shapes = operand_shapes(groups * in_group, n_tm * chunks * rows)
        scratch += [pltpu.VMEM(shape, jnp.bfloat16) for shape in shapes]
    return pl.pallas_call(
        functools.partial(correlate_kernel, frames, prepared),
        out_shape=jax.ShapeDtypeStruct((npairs, TILE, 2 * TILE), jnp.bfloat16),
        in_specs=[
            pl.BlockSpec(memory_space=pltpu.SMEM),
            *[pl.BlockSpec(memory_space=pltpu.VMEM)] * len(operands),
        ],
        out_specs=pl.BlockSpec(memory_space=pltpu.HBM),
        scratch_shapes=scratch,
        compiler_params=pltpu.CompilerParams(vmem_limit_bytes=VMEM_LIMIT),
        name="correlate",
    )(pltpu.with_memory_space_constraint(pairs, pltpu.SMEM), *operands)


def shards(voltages, channels, tile_pairs):
    n_wide = lax.axis_size("wide")
    n_tm = lax.axis_size("tm")
    in_dev = voltages.shape[0]
    frames_all = voltages.shape[1] // NFFT * n_tm
    per_dev = channels.shape[0] // (n_wide * n_tm)
    prepared = per_dev == 1 and in_dev % LANES == 0
    *made, pairs = transform(voltages, channels, tile_pairs.T, n_wide, n_tm, prepared)
    if prepared:
        return correlate(made, pairs, frames_all, True)[None]
    visibility = []
    for s in range(per_dev):
        spectra = made[0][:, :, :, s]
        if in_dev % TILE:
            chunks, rows = spectra.shape[2:4]
            spectra = spectra.transpose(1, 2, 3, 0, 4).reshape(1, n_tm, chunks, rows, n_wide * in_dev)
        visibility.append(correlate([spectra], pairs, frames_all, False))
    return jnp.stack(visibility)


def solution(mesh):
    mapped = jax.shard_map(
        shards,
        mesh=mesh,
        in_specs=(P("wide", ("grp", "tm")), P(), P()),
        out_specs=P(("grp", "wide", "tm"), None, None, None),
        check_vma=False,
    )

    def traced(*args):
        with jax.sharding.use_abstract_mesh(mesh.abstract_mesh):
            return mapped(*args)

    return traced
```

```python
import functools

import jax
import jax.numpy as jnp
from jax import lax
from jax.experimental import pallas as pl
from jax.experimental.pallas import tpu as pltpu
from jax.sharding import PartitionSpec as P

TILE = 64
NFFT = 2048
LANES = 128
SUBLANES = 8
UNROLL = 16
GROUP = 2
MXU = 256
MAXCHUNKS = 1
CHUNK = 4
LAG = 4
VMEM_LIMIT = 40 << 20
MESH = pl.DeviceIdType.MESH


def cos_sin(multiplier, steps):
    phase = lax.rem(multiplier * steps, NFFT)
    angle = (2.0 * jnp.pi / NFFT) * phase.astype(jnp.float32)
    return jnp.cos(angle), jnp.sin(angle)


def fill_table(channels_ref, table):
    count = channels_ref.shape[1]
    highs = NFFT // LANES
    scale = 1.0 / jnp.sqrt(jnp.float32(0.375 * NFFT))
    square = (count, count)
    diagonal = lax.broadcasted_iota(jnp.int32, square, 0) == lax.broadcasted_iota(jnp.int32, square, 1)
    row = jnp.broadcast_to(channels_ref[...].astype(jnp.float32), square)
    channels = jnp.sum(jnp.where(diagonal, row, 0.0), axis=1, keepdims=True).astype(jnp.int32)
    low = lax.broadcasted_iota(jnp.int32, (count, LANES), 1)
    low_cos, low_sin = cos_sin(channels, low)
    high_cos, high_sin = cos_sin(channels, LANES * low)
    win_low = lax.broadcasted_iota(jnp.int32, (8, LANES), 1)
    win_cos, win_sin = cos_sin(1, win_low)
    win_high_cos, win_high_sin = cos_sin(1, LANES * win_low)
    for high in range(highs):
        columns = slice(high * LANES, (high + 1) * LANES)
        wc, ws = win_high_cos[:, high : high + 1], win_high_sin[:, high : high + 1]
        window = (0.5 - 0.5 * (win_cos * wc - win_sin * ws)) * scale
        window = jnp.broadcast_to(window[:1], (count, LANES))
        hc, hs = high_cos[:, high : high + 1], high_sin[:, high : high + 1]
        real = window * (low_cos * hc - low_sin * hs)
        imag = -window * (low_sin * hc + low_cos * hs)
        table[:, columns] = jnp.concatenate([real, imag], 0).astype(jnp.bfloat16)


def transformed(table, block):
    return lax.dot_general(
        table[...], block[...], (((1,), (1,)), ((), ())), preferred_element_type=jnp.float32
    )


def transform_kernel(n_wide, n_tm, prepared, channels_hbm, v_hbm, pairs_hbm, *refs):
    if prepared:
        left, right, pairs, turned, *scratch = refs
    else:
        turned, pairs, *scratch = refs
    channels, blocks, table, staged, send, sems = scratch
    frames, in_dev, _ = blocks.shape
    chunks, count, rows, _ = send.shape
    part = frames // chunks
    group = GROUP if part % GROUP == 0 else 1
    wide, tm = lax.axis_index("wide"), lax.axis_index("tm")
    me = wide * n_tm + tm
    peers = n_wide * n_tm
    per_dev = count // peers
    batch = batch_of(n_wide)

    def arrived(stage):
        return sems.at[frames + 1 + stage]

    fetch = pltpu.make_async_copy(channels_hbm, channels, sems.at[frames])
    fetch.start()
    loads = [
        pltpu.make_async_copy(v_hbm.at[:, pl.ds(f * NFFT, NFFT)], blocks.at[f], sems.at[f])
        for f in range(frames)
    ]
    for load in loads:
        load.start()

    def device(peer):
        return {"wide": peer // n_tm, "tm": lax.rem(peer, n_tm)}

    barrier = pltpu.get_barrier_semaphore()

    def greet(k, carry):
        peer = lax.rem(me + k, peers)
        pl.semaphore_signal(barrier, inc=1, device_id=device(peer), device_id_type=MESH)
        return carry

    lax.fori_loop(1, peers, greet, 0)

    fetch.wait()
    fetch_pairs = pltpu.make_async_copy(pairs_hbm, pairs, sems.at[frames])
    fetch_pairs.start()
    fill_table(channels, table)

    upper = 2 * wide // n_wide
    own_turn = upper * me + (1 - upper) * (peers - 1 - me)

    def peer_at(k):
        turn = k + (k + peers - own_turn) // peers
        return upper * turn + (1 - upper) * (peers - 1 - turn)

    def round_for(c, peer):
        span = pl.ds(peer * per_dev, per_dev)
        return send.at[c, span]

    def finish(f, values):
        c, row = f // part, f % part
        for q in range(2):
            staged[c, :, q * part + row, :] = values[q * count : (q + 1) * count]
        if row < part - 1:
            return
        send[c] = staged[c].astype(jnp.bfloat16)
        if c == 0:
            fetch_pairs.wait()
            pl.semaphore_wait(barrier, peers - 1)

        def start(k, carry):
            peer = peer_at(k)
            pltpu.make_async_remote_copy(
                src_ref=round_for(c, peer),
                dst_ref=turned.at[wide, tm, c],
                send_sem=sems.at[frames],
                recv_sem=arrived(wide // batch),
                device_id=device(peer),
                device_id_type=MESH,
            ).start()
            return carry

        lax.fori_loop(0, peers - 1, start, 0, unroll=peers <= UNROLL)
        pltpu.make_async_copy(round_for(c, me), turned.at[wide, tm, c], arrived(wide // batch)).start()

    if in_dev == MXU:

        def pipelined(*sums):
            def pop(f):
                return pltpu.matmul_pop(sums[f % 2]) + pltpu.matmul_pop(sums[2 + f % 2])

            for f in range(frames):
                loads[f].wait()
                for k in range(NFFT // MXU):
                    unit, slot = k % 2, k // 2 % 2
                    columns = slice(k * MXU, (k + 1) * MXU)
                    pltpu.matmul_push_rhs(blocks[f, :, columns], slot, unit, transpose=True)
                    pltpu.matmul_acc_lhs(sums[2 * unit + f % 2], table[:, columns], load_staged_rhs=slot)
                if f:
                    finish(f - 1, pop(f - 1))
            finish(frames - 1, pop(frames - 1))

        sums = [pltpu.ACC(unit)((2 * count, in_dev), jnp.float32) for unit in (0, 0, 1, 1)]
        pl.run_scoped(pipelined, *sums)
    else:
        for f0 in range(0, frames, group):
            members = range(f0, f0 + group)
            for f in members:
                loads[f].wait()
            spectrum = [transformed(table, blocks.at[f]) for f in members]
            for f, values in zip(members, spectrum):
                finish(f, values)

    others = send.at[:, pl.ds(0, (peers - 1) * per_dev)]
    pltpu.make_async_copy(others, others, sems.at[frames]).wait()

    def arrive(step, carry):
        stage = upper * (n_wide // batch - 1 - step) + (1 - upper) * step
        landed = turned.at[pl.ds(stage * batch, batch)]
        pltpu.make_async_copy(landed, landed, arrived(stage)).wait()
        if prepared:
            for g in range(batch):
                g = stage * batch + g
                prepare([turned[g, t, c, 0] for t in range(n_tm) for c in range(chunks)], left, right, g)
        return carry

    lax.fori_loop(0, n_wide // batch, arrive, 0, unroll=n_wide // batch <= UNROLL)


def batch_of(n_wide):
    return 2 if n_wide % 2 == 0 else 1


def prepare(blocks, left, right, g):
    rows, in_group = blocks[0].shape
    half = rows // 2
    plain = jnp.concatenate(blocks, 0)
    swapped = jnp.concatenate([x for b in blocks for x in (b[half:], -b[:half])], 0)
    span = pl.ds(pl.multiple_of(g * in_group, in_group), in_group)
    left[span, :] = plain.T
    for j in range(in_group // TILE):
        columns = slice(j * TILE, (j + 1) * TILE)
        both = jnp.concatenate([plain[:, columns], swapped[:, columns]], 1)
        right[g * (in_group // TILE) + j] = both


def operand_shapes(inputs, depth):
    return (inputs, depth), (inputs // TILE, depth, 2 * TILE)


def transform(voltages, channels, pairs, n_wide, n_tm, prepared):
    in_dev, samples = voltages.shape
    frames = samples // NFFT
    count = channels.shape[0]
    peers = n_wide * n_tm
    chunks = min(MAXCHUNKS, max(1, 2 * frames // SUBLANES))
    rows = 2 * frames // chunks
    turned = pltpu.VMEM((n_wide, n_tm, chunks, count // peers, rows, in_dev), jnp.bfloat16)
    made = [turned]
    if prepared:
        made = [
            pltpu.VMEM(shape, jnp.bfloat16)
            for shape in operand_shapes(n_wide * in_dev, 2 * frames * n_tm)
        ]
    inputs = channels.reshape(1, count), voltages, pairs
    return pl.pallas_call(
        functools.partial(transform_kernel, n_wide, n_tm, prepared),
        out_shape=(*made, pltpu.SMEM(pairs.shape, jnp.int32)),
        in_specs=[pl.BlockSpec(memory_space=pltpu.HBM)] * 3,
        out_specs=(
            *[pl.BlockSpec(memory_space=pltpu.VMEM)] * len(made),
            pl.BlockSpec(memory_space=pltpu.SMEM),
        ),
        scratch_shapes=[
            *([turned] if prepared else []),
            pltpu.VMEM((1, count), jnp.int32),
            pltpu.VMEM((frames, in_dev, NFFT), jnp.bfloat16),
            pltpu.VMEM((2 * count, NFFT), jnp.bfloat16),
            pltpu.VMEM((chunks, count, rows, in_dev), jnp.float32),
            pltpu.VMEM((chunks, count, rows, in_dev), jnp.bfloat16),
            pltpu.SemaphoreType.DMA((frames + 1 + n_wide // batch_of(n_wide),)),
        ],
        compiler_params=pltpu.CompilerParams(
            collective_id=0, has_side_effects=True, vmem_limit_bytes=VMEM_LIMIT
        ),
        name="transform",
    )(*[pltpu.with_memory_space_constraint(x, pltpu.HBM) for x in inputs])


def correlate_kernel(frames, prepared, pairs_ref, *refs):
    if prepared:
        left, right, out, products, sem = refs
    else:
        spectra, out, products, sem, left, right = refs
        groups, n_tm, parts, _, _ = spectra.shape
        for g in range(groups):
            prepare([spectra[g, t, c] for t in range(n_tm) for c in range(parts)], left, right, g)
    npairs = out.shape[0]
    waiting = []

    def store():
        p, sums = waiting.pop(0)
        products[p] = (sums * (1.0 / frames)).astype(jnp.bfloat16)
        if (p + 1) % CHUNK == 0 or p + 1 == npairs:
            start = p // CHUNK * CHUNK
            span = pl.ds(start, p + 1 - start)
            pltpu.make_async_copy(products.at[span], out.at[span], sem).start()

    for p in range(npairs):
        first = left[pl.ds(pl.multiple_of(pairs_ref[0, p] * TILE, TILE), TILE), :]
        second = right[pairs_ref[1, p]]
        waiting.append((p, jnp.dot(first, second, preferred_element_type=jnp.float32)))
        if p >= LAG:
            store()
    while waiting:
        store()
    pltpu.make_async_copy(products, out, sem).wait()


def correlate(operands, pairs, frames, prepared):
    npairs = pairs.shape[1]
    scratch = [
        pltpu.VMEM((npairs, TILE, 2 * TILE), jnp.bfloat16),
        pltpu.SemaphoreType.DMA,
    ]
    if not prepared:
        groups, n_tm, chunks, rows, in_group = operands[0].shape
        shapes = operand_shapes(groups * in_group, n_tm * chunks * rows)
        scratch += [pltpu.VMEM(shape, jnp.bfloat16) for shape in shapes]
    return pl.pallas_call(
        functools.partial(correlate_kernel, frames, prepared),
        out_shape=jax.ShapeDtypeStruct((npairs, TILE, 2 * TILE), jnp.bfloat16),
        in_specs=[
            pl.BlockSpec(memory_space=pltpu.SMEM),
            *[pl.BlockSpec(memory_space=pltpu.VMEM)] * len(operands),
        ],
        out_specs=pl.BlockSpec(memory_space=pltpu.HBM),
        scratch_shapes=scratch,
        compiler_params=pltpu.CompilerParams(vmem_limit_bytes=VMEM_LIMIT),
        name="correlate",
    )(pltpu.with_memory_space_constraint(pairs, pltpu.SMEM), *operands)


def shards(voltages, channels, tile_pairs):
    n_wide = lax.axis_size("wide")
    n_tm = lax.axis_size("tm")
    in_dev = voltages.shape[0]
    frames_all = voltages.shape[1] // NFFT * n_tm
    per_dev = channels.shape[0] // (n_wide * n_tm)
    prepared = per_dev == 1 and in_dev % LANES == 0
    *made, pairs = transform(voltages, channels, tile_pairs.T, n_wide, n_tm, prepared)
    if prepared:
        return correlate(made, pairs, frames_all, True)[None]
    visibility = []
    for s in range(per_dev):
        spectra = made[0][:, :, :, s]
        if in_dev % TILE:
            chunks, rows = spectra.shape[2:4]
            spectra = spectra.transpose(1, 2, 3, 0, 4).reshape(1, n_tm, chunks, rows, n_wide * in_dev)
        visibility.append(correlate([spectra], pairs, frames_all, False))
    return jnp.stack(visibility)


def solution(mesh):
    mapped = jax.shard_map(
        shards,
        mesh=mesh,
        in_specs=(P("wide", ("grp", "tm")), P(), P()),
        out_specs=P(("grp", "wide", "tm"), None, None, None),
        check_vma=False,
    )

    def traced(*args):
        with jax.sharding.use_abstract_mesh(mesh.abstract_mesh):
            return mapped(*args)

    return traced
```

```python
import functools

import jax
import jax.numpy as jnp
from jax import lax
from jax.experimental import pallas as pl
from jax.experimental.pallas import tpu as pltpu
from jax.sharding import PartitionSpec as P

TILE = 64
NFFT = 2048
LANES = 128
SUBLANES = 8
UNROLL = 16
GROUP = 2
MXU = 256
MAXCHUNKS = 1
CHUNK = 8
LAG = 4
VMEM_LIMIT = 40 << 20
MESH = pl.DeviceIdType.MESH


def cos_sin(multiplier, steps):
    phase = lax.rem(multiplier * steps, NFFT)
    angle = (2.0 * jnp.pi / NFFT) * phase.astype(jnp.float32)
    return jnp.cos(angle), jnp.sin(angle)


def fill_table(channels_ref, table):
    count = channels_ref.shape[1]
    highs = NFFT // LANES
    scale = 1.0 / jnp.sqrt(jnp.float32(0.375 * NFFT))
    square = (count, count)
    diagonal = lax.broadcasted_iota(jnp.int32, square, 0) == lax.broadcasted_iota(jnp.int32, square, 1)
    row = jnp.broadcast_to(channels_ref[...].astype(jnp.float32), square)
    channels = jnp.sum(jnp.where(diagonal, row, 0.0), axis=1, keepdims=True).astype(jnp.int32)
    low = lax.broadcasted_iota(jnp.int32, (count, LANES), 1)
    low_cos, low_sin = cos_sin(channels, low)
    high_cos, high_sin = cos_sin(channels, LANES * low)
    win_low = lax.broadcasted_iota(jnp.int32, (8, LANES), 1)
    win_cos, win_sin = cos_sin(1, win_low)
    win_high_cos, win_high_sin = cos_sin(1, LANES * win_low)
    for high in range(highs):
        columns = slice(high * LANES, (high + 1) * LANES)
        wc, ws = win_high_cos[:, high : high + 1], win_high_sin[:, high : high + 1]
        window = (0.5 - 0.5 * (win_cos * wc - win_sin * ws)) * scale
        window = jnp.broadcast_to(window[:1], (count, LANES))
        hc, hs = high_cos[:, high : high + 1], high_sin[:, high : high + 1]
        real = window * (low_cos * hc - low_sin * hs)
        imag = -window * (low_sin * hc + low_cos * hs)
        table[:, columns] = jnp.concatenate([real, imag], 0).astype(jnp.bfloat16)


def transformed(table, block):
    return lax.dot_general(
        table[...], block[...], (((1,), (1,)), ((), ())), preferred_element_type=jnp.float32
    )


def transform_kernel(n_wide, n_tm, prepared, channels_hbm, v_hbm, pairs_hbm, *refs):
    if prepared:
        left, right, pairs, turned, *scratch = refs
    else:
        turned, pairs, *scratch = refs
    channels, blocks, table, staged, send, sems = scratch
    frames, in_dev, _ = blocks.shape
    chunks, count, rows, _ = send.shape
    part = frames // chunks
    group = GROUP if part % GROUP == 0 else 1
    wide, tm = lax.axis_index("wide"), lax.axis_index("tm")
    me = wide * n_tm + tm
    peers = n_wide * n_tm
    per_dev = count // peers
    batch = batch_of(n_wide)

    def arrived(stage):
        return sems.at[frames + 1 + stage]

    fetch = pltpu.make_async_copy(channels_hbm, channels, sems.at[frames])
    fetch.start()
    loads = [
        pltpu.make_async_copy(v_hbm.at[:, pl.ds(f * NFFT, NFFT)], blocks.at[f], sems.at[f])
        for f in range(frames)
    ]
    for load in loads:
        load.start()

    def device(peer):
        return {"wide": peer // n_tm, "tm": lax.rem(peer, n_tm)}

    barrier = pltpu.get_barrier_semaphore()

    def greet(k, carry):
        peer = lax.rem(me + k, peers)
        pl.semaphore_signal(barrier, inc=1, device_id=device(peer), device_id_type=MESH)
        return carry

    lax.fori_loop(1, peers, greet, 0)

    fetch.wait()
    fetch_pairs = pltpu.make_async_copy(pairs_hbm, pairs, sems.at[frames])
    fetch_pairs.start()
    fill_table(channels, table)

    upper = 2 * wide // n_wide
    own_turn = upper * me + (1 - upper) * (peers - 1 - me)

    def peer_at(k):
        turn = k + (k + peers - own_turn) // peers
        return upper * turn + (1 - upper) * (peers - 1 - turn)

    def round_for(c, peer):
        span = pl.ds(peer * per_dev, per_dev)
        return send.at[c, span]

    def finish(f, values):
        c, row = f // part, f % part
        for q in range(2):
            staged[c, :, q * part + row, :] = values[q * count : (q + 1) * count]
        if row < part - 1:
            return
        send[c] = staged[c].astype(jnp.bfloat16)
        if c == 0:
            fetch_pairs.wait()
            pl.semaphore_wait(barrier, peers - 1)

        def start(k, carry):
            peer = peer_at(k)
            pltpu.make_async_remote_copy(
                src_ref=round_for(c, peer),
                dst_ref=turned.at[wide, tm, c],
                send_sem=sems.at[frames],
                recv_sem=arrived(wide // batch),
                device_id=device(peer),
                device_id_type=MESH,
            ).start()
            return carry

        lax.fori_loop(0, peers - 1, start, 0, unroll=peers <= UNROLL)
        pltpu.make_async_copy(round_for(c, me), turned.at[wide, tm, c], arrived(wide // batch)).start()

    if in_dev == MXU:

        def pipelined(*sums):
            def pop(f):
                return pltpu.matmul_pop(sums[f % 2]) + pltpu.matmul_pop(sums[2 + f % 2])

            for f in range(frames):
                loads[f].wait()
                for k in range(NFFT // MXU):
                    unit, slot = k % 2, k // 2 % 2
                    columns = slice(k * MXU, (k + 1) * MXU)
                    pltpu.matmul_push_rhs(blocks[f, :, columns], slot, unit, transpose=True)
                    pltpu.matmul_acc_lhs(sums[2 * unit + f % 2], table[:, columns], load_staged_rhs=slot)
                if f:
                    finish(f - 1, pop(f - 1))
            finish(frames - 1, pop(frames - 1))

        sums = [pltpu.ACC(unit)((2 * count, in_dev), jnp.float32) for unit in (0, 0, 1, 1)]
        pl.run_scoped(pipelined, *sums)
    else:
        for f0 in range(0, frames, group):
            members = range(f0, f0 + group)
            for f in members:
                loads[f].wait()
            spectrum = [transformed(table, blocks.at[f]) for f in members]
            for f, values in zip(members, spectrum):
                finish(f, values)

    others = send.at[:, pl.ds(0, (peers - 1) * per_dev)]
    pltpu.make_async_copy(others, others, sems.at[frames]).wait()

    def arrive(step, carry):
        stage = upper * (n_wide // batch - 1 - step) + (1 - upper) * step
        landed = turned.at[pl.ds(stage * batch, batch)]
        pltpu.make_async_copy(landed, landed, arrived(stage)).wait()
        if prepared:
            for g in range(batch):
                g = stage * batch + g
                prepare([turned[g, t, c, 0] for t in range(n_tm) for c in range(chunks)], left, right, g)
        return carry

    lax.fori_loop(0, n_wide // batch, arrive, 0, unroll=n_wide // batch <= UNROLL)


def batch_of(n_wide):
    return 2 if n_wide % 2 == 0 else 1


def prepare(blocks, left, right, g):
    rows, in_group = blocks[0].shape
    half = rows // 2
    plain = jnp.concatenate(blocks, 0)
    swapped = jnp.concatenate([x for b in blocks for x in (b[half:], -b[:half])], 0)
    span = pl.ds(pl.multiple_of(g * in_group, in_group), in_group)
    left[span, :] = plain.T
    for j in range(in_group // TILE):
        columns = slice(j * TILE, (j + 1) * TILE)
        both = jnp.concatenate([plain[:, columns], swapped[:, columns]], 1)
        right[g * (in_group // TILE) + j] = both


def operand_shapes(inputs, depth):
    return (inputs, depth), (inputs // TILE, depth, 2 * TILE)


def transform(voltages, channels, pairs, n_wide, n_tm, prepared):
    in_dev, samples = voltages.shape
    frames = samples // NFFT
    count = channels.shape[0]
    peers = n_wide * n_tm
    chunks = min(MAXCHUNKS, max(1, 2 * frames // SUBLANES))
    rows = 2 * frames // chunks
    turned = pltpu.VMEM((n_wide, n_tm, chunks, count // peers, rows, in_dev), jnp.bfloat16)
    made = [turned]
    if prepared:
        made = [
            pltpu.VMEM(shape, jnp.bfloat16)
            for shape in operand_shapes(n_wide * in_dev, 2 * frames * n_tm)
        ]
    inputs = channels.reshape(1, count), voltages, pairs
    return pl.pallas_call(
        functools.partial(transform_kernel, n_wide, n_tm, prepared),
        out_shape=(*made, pltpu.SMEM(pairs.shape, jnp.int32)),
        in_specs=[pl.BlockSpec(memory_space=pltpu.HBM)] * 3,
        out_specs=(
            *[pl.BlockSpec(memory_space=pltpu.VMEM)] * len(made),
            pl.BlockSpec(memory_space=pltpu.SMEM),
        ),
        scratch_shapes=[
            *([turned] if prepared else []),
            pltpu.VMEM((1, count), jnp.int32),
            pltpu.VMEM((frames, in_dev, NFFT), jnp.bfloat16),
            pltpu.VMEM((2 * count, NFFT), jnp.bfloat16),
            pltpu.VMEM((chunks, count, rows, in_dev), jnp.float32),
            pltpu.VMEM((chunks, count, rows, in_dev), jnp.bfloat16),
            pltpu.SemaphoreType.DMA((frames + 1 + n_wide // batch_of(n_wide),)),
        ],
        compiler_params=pltpu.CompilerParams(
            collective_id=0, has_side_effects=True, vmem_limit_bytes=VMEM_LIMIT
        ),
        name="transform",
    )(*[pltpu.with_memory_space_constraint(x, pltpu.HBM) for x in inputs])


def correlate_kernel(frames, prepared, pairs_ref, *refs):
    if prepared:
        left, right, out, products, sem = refs
    else:
        spectra, out, products, sem, left, right = refs
        groups, n_tm, parts, _, _ = spectra.shape
        for g in range(groups):
            prepare([spectra[g, t, c] for t in range(n_tm) for c in range(parts)], left, right, g)
    npairs = out.shape[0]
    waiting = []

    def store():
        p, sums = waiting.pop(0)
        products[p] = (sums * (1.0 / frames)).astype(jnp.bfloat16)
        if (p + 1) % CHUNK == 0 or p + 1 == npairs:
            start = p // CHUNK * CHUNK
            span = pl.ds(start, p + 1 - start)
            pltpu.make_async_copy(products.at[span], out.at[span], sem).start()

    for p in range(npairs):
        first = left[pl.ds(pl.multiple_of(pairs_ref[0, p] * TILE, TILE), TILE), :]
        second = right[pairs_ref[1, p]]
        waiting.append((p, jnp.dot(first, second, preferred_element_type=jnp.float32)))
        if p >= LAG:
            store()
    while waiting:
        store()
    pltpu.make_async_copy(products, out, sem).wait()


def correlate(operands, pairs, frames, prepared):
    npairs = pairs.shape[1]
    scratch = [
        pltpu.VMEM((npairs, TILE, 2 * TILE), jnp.bfloat16),
        pltpu.SemaphoreType.DMA,
    ]
    if not prepared:
        groups, n_tm, chunks, rows, in_group = operands[0].shape
        shapes = operand_shapes(groups * in_group, n_tm * chunks * rows)
        scratch += [pltpu.VMEM(shape, jnp.bfloat16) for shape in shapes]
    return pl.pallas_call(
        functools.partial(correlate_kernel, frames, prepared),
        out_shape=jax.ShapeDtypeStruct((npairs, TILE, 2 * TILE), jnp.bfloat16),
        in_specs=[
            pl.BlockSpec(memory_space=pltpu.SMEM),
            *[pl.BlockSpec(memory_space=pltpu.VMEM)] * len(operands),
        ],
        out_specs=pl.BlockSpec(memory_space=pltpu.HBM),
        scratch_shapes=scratch,
        compiler_params=pltpu.CompilerParams(vmem_limit_bytes=VMEM_LIMIT),
        name="correlate",
    )(pltpu.with_memory_space_constraint(pairs, pltpu.SMEM), *operands)


def shards(voltages, channels, tile_pairs):
    n_wide = lax.axis_size("wide")
    n_tm = lax.axis_size("tm")
    in_dev = voltages.shape[0]
    frames_all = voltages.shape[1] // NFFT * n_tm
    per_dev = channels.shape[0] // (n_wide * n_tm)
    prepared = per_dev == 1 and in_dev % LANES == 0
    *made, pairs = transform(voltages, channels, tile_pairs.T, n_wide, n_tm, prepared)
    if prepared:
        return correlate(made, pairs, frames_all, True)[None]
    visibility = []
    for s in range(per_dev):
        spectra = made[0][:, :, :, s]
        if in_dev % TILE:
            chunks, rows = spectra.shape[2:4]
            spectra = spectra.transpose(1, 2, 3, 0, 4).reshape(1, n_tm, chunks, rows, n_wide * in_dev)
        visibility.append(correlate([spectra], pairs, frames_all, False))
    return jnp.stack(visibility)


def solution(mesh):
    mapped = jax.shard_map(
        shards,
        mesh=mesh,
        in_specs=(P("wide", ("grp", "tm")), P(), P()),
        out_specs=P(("grp", "wide", "tm"), None, None, None),
        check_vma=False,
    )

    def traced(*args):
        with jax.sharding.use_abstract_mesh(mesh.abstract_mesh):
            return mapped(*args)

    return traced
```
